32 devices in a mesh: leaf: 16 (over z, y, x), front: 2 (over core).
Axes of the slice: x: 2, y: 2, z: 4, core: 2. Of those that a mesh axis runs over, the one named last changes fastest.
Arguments:
- child_fronts: float32 [48, 2, 512, 1024], P('leaf', None, 'front'), may hold values from 0 to 16, as said below
- child_live: int32 [16], P('leaf'), may hold values from 1 to 3, as said below
- row_map: int32 [48, 4], P('leaf'), may hold values from 0 to 7, as said below
- parent_fronts: float32 [16, 2, 256, 1024], P('leaf', None, 'front'), may hold values from 0 to 16, as said below
Outputs:
- child_panels: float32 [48, 2, 512, 512], P('leaf', None, 'front')
- parent_panels: float32 [16, 2, 256, 512], P('leaf', None, 'front')
- parent_updates: float32 [16, 256, 512], P('leaf', 'front')
The draws below stay inside these ranges and needn't reach their ends.
Inputs may be any that keep to these rules, and one draw needn't show every extreme that they name: `child_fronts`: each front and each separator front is symmetric, and it and every separator front after the extend-add are positive definite. `parent_fronts`: symmetric as the child fronts. `child_live`: the two subtrees of leaf indices 2 * k and 2 * k + 1 hold at most 4 live fronts together; in every draw some subtree holds 3. `row_map`: each row names 4 different blocks of the separator, in increasing order.
All inputs are finite; a program needn't handle non-finite values.
Results may differ from the reference program's by a relative error of at most 0.000053.
Values sent between devices are 32-bit elements; how exact they have to be, the bound alone decides.
A program may use at most 128 MiB of HBM per device.

```python
import jax
import jax.numpy as jnp
from jax import lax

FC = 1024
PIV = 512
FP = 1024
PPIV = 512
BLK = 128
CBLK = 4
SLOTS = 3
N_LEAF = 16


def symmetric_fronts(key, number, extent):
    front_keys = jax.random.split(key, number)

    def one_front(front_key):
        key_points, key_diagonal = jax.random.split(front_key, 2)
        points = jax.random.uniform(key_points, (extent, 3), jnp.float32, 0.0, 1.0)
        squares = jnp.sum(points * points, axis=1)
        inner = jnp.dot(points, points.T, precision=lax.Precision.HIGHEST)
        distance = jnp.sqrt(jnp.maximum(squares[:, None] + squares[None, :] - 2.0 * inner, 0.0))
        reach = 0.5 * extent ** (-1.0 / 3.0)
        kernel = jnp.exp(-distance / reach)
        kernel = 0.5 * (kernel + kernel.T)
        identity = jnp.eye(extent, dtype=jnp.float32)
        diagonal = jax.random.uniform(key_diagonal, (extent,), jnp.float32, 0.5, 1.5)
        matrix = kernel * (1.0 - identity) + (1.0 + diagonal)[:, None] * identity
        return matrix
    return lax.map(one_front, front_keys)


def draw_child_fronts(key, part):
    matrix = symmetric_fronts(jax.random.fold_in(key, 3), N_LEAF * SLOTS, FC)
    return matrix.reshape(N_LEAF * SLOTS, 2, FC // 2, FC)


def draw_parent_fronts(key, part):
    matrix = symmetric_fronts(jax.random.fold_in(key, 7), N_LEAF // 2, FP)
    matrix = matrix.reshape(N_LEAF // 2, 2, 2, FP // 4, FP).transpose(0, 2, 1, 3, 4)
    return matrix.reshape(N_LEAF, 2, FP // 4, FP)


def draw_child_live(key, part):
    pair_count = N_LEAF // 2
    key_heavy, key_other, key_flip, key_force = jax.random.split(jax.random.fold_in(key, 11), 4)
    heavy = jax.random.randint(key_heavy, (pair_count,), 0, 4) == 0
    forced = jax.random.randint(key_force, (), 0, pair_count)
    heavy = heavy | (jnp.arange(pair_count) == forced)
    partner = jax.random.randint(key_other, (pair_count,), 1, 3)
    first_chip = jnp.where(heavy, SLOTS, 1)
    second_chip = jnp.where(heavy, 1, partner)
    flipped = jax.random.randint(key_flip, (pair_count,), 0, 2) == 1
    even_chip = jnp.where(flipped, second_chip, first_chip)
    odd_chip = jnp.where(flipped, first_chip, second_chip)
    return jnp.stack([even_chip, odd_chip], axis=1).reshape(N_LEAF).astype(jnp.int32)


def draw_row_map(key, part):
    number = N_LEAF * SLOTS
    blocks = FP // BLK
    scores = jax.random.randint(jax.random.fold_in(key, 13), (number, blocks), 0, 1 << 20) * blocks + jnp.arange(blocks, dtype=jnp.int32)[None, :]
    chosen = jnp.argsort(scores, axis=1)[:, :FC // 2 // BLK]
    return jnp.sort(chosen, axis=1).astype(jnp.int32)


def setup_inputs(seed: int = 0) -> dict:
    seeds = jax.random.split(jax.random.key(seed), 5)
    child_fronts = draw_child_fronts(jax.random.fold_in(seeds[4], 71), 0)
    child_live = draw_child_live(jax.random.fold_in(seeds[4], 71), 0)
    row_map = draw_row_map(jax.random.fold_in(seeds[4], 71), 0)
    parent_fronts = draw_parent_fronts(jax.random.fold_in(seeds[4], 71), 0)
    return {"child_fronts": child_fronts, "child_live": child_live, "row_map": row_map, "parent_fronts": parent_fronts}


highest = lax.Precision.HIGHEST

def partial_factor(matrix, pivots):
    factor = jnp.linalg.cholesky(matrix[:pivots, :pivots])
    lower_panel = jax.scipy.linalg.solve_triangular(factor, matrix[pivots:, :pivots].T, lower=True).T
    update = matrix[pivots:, pivots:] - jnp.dot(lower_panel.astype(jnp.float32), lower_panel.T.astype(jnp.float32), precision=highest, preferred_element_type=jnp.float32)
    return (jnp.concatenate([factor, lower_panel], axis=0), update)

def reference(child_fronts, child_live, row_map, parent_fronts):
    total_fronts = N_LEAF * SLOTS
    fronts = child_fronts.reshape(total_fronts, FC, FC)
    slot_ids = jnp.arange(total_fronts, dtype=jnp.int32) % SLOTS
    active = slot_ids < jnp.repeat(child_live, SLOTS)

    def one_child(operands):
        matrix, is_live = operands
        panel_rows, update = partial_factor(matrix, PIV)
        return (jnp.where(is_live, panel_rows, 0.0), jnp.where(is_live, update, 0.0))
    panels, updates = lax.map(one_child, (fronts, active))
    child_panels = panels.reshape(total_fronts, 2, PIV, PIV)
    pair_count = N_LEAF // 2
    parent_blocks = FP // BLK
    parents = parent_fronts.reshape(pair_count, 2, 2, FP // 4, FP).transpose(0, 2, 1, 3, 4).reshape(pair_count, FP, FP)
    block_hot = (row_map[:, :, None] == jnp.arange(parent_blocks, dtype=jnp.int32)[None, None, :]).astype(jnp.float32)
    hot_pairs = block_hot.reshape(pair_count, 2 * SLOTS, CBLK, parent_blocks)
    tile_view = updates.reshape(pair_count, 2 * SLOTS, CBLK, BLK, CBLK, BLK)

    def one_parent(operands):
        parent, tile_block, hot_block = operands
        spread = jnp.einsum('karbs,kbp->karps', tile_block, hot_block, precision=highest)
        assembled = jnp.einsum('karps,kaq->qrps', spread, hot_block, precision=highest).reshape(FP, FP)
        return partial_factor(parent + assembled, PPIV)
    parent_panels_all, parent_updates_all = lax.map(one_parent, (parents, tile_view, hot_pairs))
    parent_panels = parent_panels_all.reshape(pair_count, 2, 2, FP // 4, PPIV).transpose(0, 2, 1, 3, 4).reshape(N_LEAF, 2, FP // 4, PPIV)
    parent_updates = parent_updates_all.reshape(N_LEAF, FP // 4, FP - PPIV)
    return (child_panels, parent_panels, parent_updates)
```

```python
import functools

import jax
import jax.numpy as jnp
from jax import lax
from jax.experimental import pallas as pl
from jax.experimental.pallas import tpu as pltpu
from jax.sharding import PartitionSpec as P

HIGHEST = lax.Precision.HIGHEST
LANES = 128
SUB = 8
GROUP = 4
VMEM_LIMIT = 60 * 1024 * 1024


def dot_nt(a, b):
    return lax.dot_general(
        a, b, (((1,), (1,)), ((), ())), precision=HIGHEST, preferred_element_type=jnp.float32
    )


def spread_lane(x, lane):
    return jnp.broadcast_to(x[:, lane : lane + 1], (SUB, LANES))


def spread_row(x, row):
    return jnp.broadcast_to(x[row : row + 1, :], (SUB, LANES))


def eliminate_group(tiles, start, lane_ids, row_ids):
    tile, first = divmod(start, SUB)
    size = GROUP
    rows = [spread_row(tiles[tile], first + k) for k in range(size)]
    entry = {}
    for k in range(size):
        for l in range(k + 1):
            entry[k, l] = spread_lane(rows[k], start + l)
    ratio = {}
    inverse = []
    for k in range(size):
        inverse.append(1.0 / entry[k, k])
        for m in range(k + 1, size):
            ratio[m, k] = entry[m, k] * inverse[k]
        for m in range(k + 1, size):
            for l in range(k + 1, m + 1):
                entry[m, l] = entry[m, l] - ratio[m, k] * entry[l, k]
    inside = (lane_ids >= start) & (lane_ids < start + size)
    for k in range(size):
        unit = jnp.where(lane_ids == start + k, 1.0, 0.0)
        rows[k] = jnp.where(inside, unit, rows[k])
    for k in range(size):
        for l in range(k):
            rows[k] = rows[k] - ratio[k, l] * rows[l]
    scaled = [rows[k] * inverse[k] for k in range(size)]
    result = list(tiles)
    for t in range(tile, len(tiles)):
        old = tiles[t]
        if t == tile and first + size == SUB:
            new = old
        else:
            factors = []
            for k in range(size):
                value = spread_lane(old, start + k)
                for l in range(k):
                    value = value - factors[l] * ratio[k, l]
                factors.append(value)
            new = jnp.where(inside, 0.0, old)
            total = factors[0] * scaled[0]
            for k in range(1, size):
                total = total + factors[k] * scaled[k]
            new = new - total
        if t == tile:
            new = jnp.where(row_ids < first, old, new)
            for k in range(size):
                root = lax.rsqrt(entry[k, k])
                new = jnp.where(row_ids == first + k, rows[k] * root, new)
        result[t] = new
    return result


def factor_inverses(blocks):
    lane_ids = lax.broadcasted_iota(jnp.int32, (SUB, LANES), 1)
    row_ids = lax.broadcasted_iota(jnp.int32, (SUB, LANES), 0)
    count = LANES // SUB
    tiles = [[b[t * SUB : (t + 1) * SUB, :] for t in range(count)] for b in blocks]
    for start in range(0, LANES, GROUP):
        tiles = [eliminate_group(t, start, lane_ids, row_ids) for t in tiles]
    rows = lax.broadcasted_iota(jnp.int32, (LANES, LANES), 0)
    columns = lax.broadcasted_iota(jnp.int32, (LANES, LANES), 1)
    return [jnp.where(columns <= rows, jnp.concatenate(t, axis=0), 0.0) for t in tiles]


def factor_panels(work, pivots):
    fronts, rows, _ = work.shape
    steps = pivots // LANES
    triangle = lax.broadcasted_iota(jnp.int32, (LANES, LANES), 1) <= lax.broadcasted_iota(
        jnp.int32, (LANES, LANES), 0
    )

    @pl.loop(0, steps)
    def _(step):
        here = pl.multiple_of(step * LANES, LANES)
        span = pl.ds(here, LANES)
        inverses = factor_inverses([work[f, span, span] for f in range(fronts)])
        for f in range(fronts):
            work[f, span, span] = jnp.where(
                triangle, dot_nt(work[f, span, span], inverses[f]), 0.0
            )

        @pl.loop(step + 1, rows // LANES)
        def _(below):
            low = pl.ds(pl.multiple_of(below * LANES, LANES), LANES)
            for f in range(fronts):
                work[f, low, span] = dot_nt(work[f, low, span], inverses[f])

        @pl.loop(step + 1, steps)
        def _(column):
            side = pl.ds(pl.multiple_of(column * LANES, LANES), LANES)
            others = [work[f, side, span] for f in range(fronts)]

            @pl.loop(column, rows // LANES)
            def _(below):
                low = pl.ds(pl.multiple_of(below * LANES, LANES), LANES)
                for f in range(fronts):
                    work[f, low, side] = work[f, low, side] - dot_nt(
                        work[f, low, span], others[f]
                    )


def clear_upper(work, pivots):
    for step in range(pivots // LANES):
        top = step * LANES
        if top + LANES < pivots:
            for f in range(work.shape[0]):
                work[f, top : top + LANES, top + LANES : pivots] = jnp.zeros(
                    (LANES, pivots - top - LANES), jnp.float32
                )


def child_kernel(place, own, other, out, work):
    core, live = place[0], place[1]
    slots, _, half, pivots = own.shape
    mine = pl.ds(pl.multiple_of(core * half, half), half)
    yours = pl.ds(pl.multiple_of((1 - core) * half, half), half)
    for s in range(slots):
        work[s, mine, :] = own[s, 0]
        work[s, yours, :] = other[s]
        work[s, 2 * half :, :] = own[s, 1]
    factor_panels(work, pivots)
    clear_upper(work, pivots)
    for s in range(slots):
        out[s, 0] = jnp.where(s < live, work[s, mine, :], 0.0)
        out[s, 1] = jnp.where(s < live, work[s, 2 * half :, :], 0.0)


def add_kernel(
    place, maps, own22, other22, own21, other21, parent, pivot_out, keep_out, send_out, whole
):
    core, live, half = place[0], place[1], place[2]
    slots, rows, width = own22.shape
    block = LANES
    per_core = rows // block
    blocks = width // block
    mine = pl.ds(pl.multiple_of(core * rows, rows), rows)
    yours = pl.ds(pl.multiple_of((1 - core) * rows, rows), rows)
    for s in range(slots):
        whole[s, mine, :] = own21[s]
        whole[s, yours, :] = other21[s]
    pivot_out[...] = jnp.zeros_like(pivot_out)
    keep_out[...] = parent[1]
    send_out[...] = jnp.zeros_like(send_out)
    pivot_out[half] = parent[0, :, : pivot_out.shape[2]]
    pivot_blocks = pivot_out.shape[2] // block

    @pl.loop(0, slots)
    def _(s):
        @pl.loop(0, blocks)
        def _(a):
            target = maps[s, a]

            @pl.when((s < live) & (target % 2 == core))
            def _():
                span = pl.ds(pl.multiple_of(a * block, block), block)
                low = pl.ds(pl.multiple_of((a % per_core) * block, block), block)
                is_mine = a // per_core == core
                source = jnp.where(is_mine, own22[s, low, :], other22[s, low, :])
                update = source - dot_nt(whole[s, span, :], whole[s])
                owner = (target // 2) % 2
                for b in range(blocks):
                    tile = update[:, b * block : (b + 1) * block]
                    column = maps[s, b]
                    there = pl.ds(pl.multiple_of(column * block, block), block)

                    @pl.when((target < pivot_blocks) & (column < pivot_blocks))
                    def _():
                        pivot_out[owner, :, there] += tile

                    @pl.when((target >= pivot_blocks) & (owner == half))
                    def _():
                        keep_out[:, there] += tile

                    @pl.when((target >= pivot_blocks) & (owner != half))
                    def _():
                        send_out[:, there] += tile


def parent_kernel(place, mine, yours, lower, out, work):
    core, half = place[0], place[2]
    _, rows, pivots = mine.shape
    for h in range(2):
        work[0, pl.ds(pl.multiple_of((2 * h + core) * rows, rows), rows), :] = mine[h]
        work[0, pl.ds(pl.multiple_of((2 * h + 1 - core) * rows, rows), rows), :] = yours[h]
    work[0, pivots:, :] = lower[...]
    factor_panels(work, pivots)
    clear_upper(work, pivots)
    out[0] = work[0, pl.ds(pl.multiple_of((2 * half + core) * rows, rows), rows), :]
    out[1] = work[0, pivots:, :]


def update_kernel(place, base, own, mate, pair, cross, out):
    core, half = place[0], place[2]
    rows = own.shape[0]
    pieces = (
        (own, 2 * half + core),
        (mate, 2 * half + 1 - core),
        (pair, 2 * (1 - half) + core),
        (cross, 2 * (1 - half) + 1 - core),
    )
    for piece, index in pieces:
        side = pl.ds(pl.multiple_of(index * rows, rows), rows)
        out[:, side] = base[:, side] - dot_nt(own[...], piece[...])


def call(kernel, shapes, scratch, scalars, *arrays):
    vmem = pl.BlockSpec(memory_space=pltpu.VMEM)
    smem = pl.BlockSpec(memory_space=pltpu.SMEM)
    many = isinstance(shapes, list)
    made = [jax.ShapeDtypeStruct(s, jnp.float32) for s in (shapes if many else [shapes])]
    return pl.pallas_call(
        kernel,
        out_shape=made if many else made[0],
        in_specs=[smem] * len(scalars) + [vmem] * len(arrays),
        out_specs=[vmem] * len(made) if many else vmem,
        scratch_shapes=[pltpu.VMEM(s, jnp.float32) for s in scratch],
        compiler_params=pltpu.CompilerParams(vmem_limit_bytes=VMEM_LIMIT),
    )(*scalars, *arrays)


def on_device(child_fronts, child_live, row_map, parent_fronts):
    slots, _, quarter, order = child_fronts.shape
    pivots = order // 2
    core = lax.axis_index("front")
    half = lax.axis_index("leaf") % 2
    place = jnp.stack([core, child_live[0], half]).astype(jnp.int32)
    other_core = [(i, i ^ 1) for i in range(lax.axis_size("front"))]
    other_chip = [(i, i ^ 1) for i in range(lax.axis_size("leaf"))]

    def mate(x):
        return lax.ppermute(x, "front", other_core)

    def pair(x):
        return lax.ppermute(x, "leaf", other_chip)

    own_panel = child_fronts[:, :, :, :pivots]
    own22 = child_fronts[:, 1, :, pivots:]
    other_pivot = mate(child_fronts[:, 0, :, :pivots])
    other22 = mate(own22)
    child_panels = call(
        child_kernel,
        (slots, 2, quarter, pivots),
        [(slots, pivots + quarter, pivots)],
        [place],
        own_panel,
        other_pivot,
    )
    own21 = child_panels[:, 1]
    other21 = mate(own21)
    rows, parent_order = parent_fronts.shape[2:]
    parent_pivots = parent_order // 2
    pivot_part, keep, send = call(
        add_kernel,
        [(2, rows, parent_pivots), (rows, parent_order), (rows, parent_order)],
        [(slots, order - pivots, pivots)],
        [place, row_map],
        own22,
        other22,
        own21,
        other21,
        parent_fronts[0],
    )
    pivot_mine = pivot_part + pair(pivot_part)
    pivot_yours = mate(pivot_mine)
    lower = keep + pair(send)
    panel = call(
        parent_kernel,
        (2, rows, parent_pivots),
        [(1, parent_pivots + rows, parent_pivots)],
        [place],
        pivot_mine,
        pivot_yours,
        lower[:, :parent_pivots],
    )
    lower21 = panel[1]
    from_pair = pair(lower21)
    update = call(
        update_kernel,
        (rows, parent_order - parent_pivots),
        [],
        [place],
        lower[:, parent_pivots:],
        lower21,
        mate(lower21),
        from_pair,
        mate(from_pair),
    )
    return child_panels, panel[None], update[None]


def solution(mesh):
    placed = (
        P("leaf", None, "front", None),
        P("leaf"),
        P("leaf", None),
        P("leaf", None, "front", None),
    )
    return jax.shard_map(
        on_device,
        mesh=mesh,
        in_specs=placed,
        out_specs=(
            P("leaf", None, "front", None),
            P("leaf", None, "front", None),
            P("leaf", "front", None),
        ),
        check_vma=False,
    )
```

```python
import functools

import jax
import jax.numpy as jnp
from jax import lax
from jax.experimental import pallas as pl
from jax.experimental.pallas import tpu as pltpu
from jax.sharding import PartitionSpec as P

LANES = 128
SUB = 8
GROUP = 4
VMEM_LIMIT = 60 * 1024 * 1024


def split(x):
    high = x.astype(jnp.bfloat16)
    return high, (x - high.astype(jnp.float32)).astype(jnp.bfloat16)


def dot_nt(a, b):
    a_high, a_low = split(a)
    b_high, b_low = split(b)
    return lax.dot_general(
        jnp.concatenate([a_high, a_high, a_low], axis=1),
        jnp.concatenate([b_high, b_low, b_high], axis=1),
        (((1,), (1,)), ((), ())),
        preferred_element_type=jnp.float32,
    )


def spread_lane(x, lane):
    return jnp.take_along_axis(x, jnp.full((SUB, LANES), lane, jnp.int32), 1, mode="promise_in_bounds")


def spread_row(x, row):
    return jnp.take_along_axis(x, jnp.full((SUB, LANES), row, jnp.int32), 0, mode="promise_in_bounds")


def eliminate_group(tiles, start, lane_ids, row_ids):
    tile, first = divmod(start, SUB)
    size = GROUP
    rows = [spread_row(tiles[tile], first + k) for k in range(size)]
    heads = [spread_lane(tiles[tile], start + k) for k in range(size)]
    entry = {}
    for k in range(size):
        for l in range(k + 1):
            entry[k, l] = spread_row(heads[l], first + k)
    ratio = {}
    inverse = []
    for k in range(size):
        inverse.append(1.0 / entry[k, k])
        for m in range(k + 1, size):
            ratio[m, k] = entry[m, k] * inverse[k]
        for m in range(k + 1, size):
            for l in range(k + 1, m + 1):
                entry[m, l] = entry[m, l] - ratio[m, k] * entry[l, k]
    inside = (lane_ids >= start) & (lane_ids < start + size)
    for k in range(size):
        unit = jnp.where(lane_ids == start + k, 1.0, 0.0)
        rows[k] = jnp.where(inside, unit, rows[k])
    for k in range(size):
        for l in range(k):
            rows[k] = rows[k] - ratio[k, l] * rows[l]
    solved = [rows[k] * inverse[k] for k in range(size)]
    for k in range(size - 2, -1, -1):
        for m in range(k + 1, size):
            solved[k] = solved[k] - ratio[m, k] * solved[m]
    result = list(tiles)
    for t in range(tile, len(tiles)):
        old = tiles[t]
        if t == tile and first + size == SUB:
            new = old
        else:
            factors = [heads[k] if t == tile else spread_lane(old, start + k) for k in range(size)]
            new = jnp.where(inside, 0.0, old)
            for k in range(size):
                new = new - factors[k] * solved[k]
        if t == tile:
            new = jnp.where(row_ids < first, old, new)
            for k in range(size):
                root = lax.rsqrt(entry[k, k])
                new = jnp.where(row_ids == first + k, rows[k] * root, new)
        result[t] = new
    return result


def factor_inverses(blocks):
    lane_ids = lax.broadcasted_iota(jnp.int32, (SUB, LANES), 1)
    row_ids = lax.broadcasted_iota(jnp.int32, (SUB, LANES), 0)
    count = LANES // SUB
    tiles = [[b[t * SUB : (t + 1) * SUB, :] for t in range(count)] for b in blocks]
    for start in range(0, LANES, GROUP):
        tiles = [eliminate_group(t, start, lane_ids, row_ids) for t in tiles]
    rows = lax.broadcasted_iota(jnp.int32, (LANES, LANES), 0)
    columns = lax.broadcasted_iota(jnp.int32, (LANES, LANES), 1)
    return [jnp.where(columns <= rows, jnp.concatenate(t, axis=0), 0.0) for t in tiles]


def factor_pivots(work, saved):
    fronts, pivots, _ = work.shape
    steps = pivots // LANES
    triangle = lax.broadcasted_iota(jnp.int32, (LANES, LANES), 1) <= lax.broadcasted_iota(
        jnp.int32, (LANES, LANES), 0
    )

    @pl.loop(0, steps)
    def _(step):
        span = pl.ds(pl.multiple_of(step * LANES, LANES), LANES)
        inverses = factor_inverses([work[f, span, span] for f in range(fronts)])
        for f in range(fronts):
            saved[f, step] = inverses[f]
            work[f, span, span] = jnp.where(
                triangle, dot_nt(work[f, span, span], inverses[f]), 0.0
            )

        @pl.loop(step + 1, steps)
        def _(below):
            low = pl.ds(pl.multiple_of(below * LANES, LANES), LANES)
            for f in range(fronts):
                work[f, low, span] = dot_nt(work[f, low, span], saved[f, step])

        @pl.loop(step + 1, steps)
        def _(column):
            side = pl.ds(pl.multiple_of(column * LANES, LANES), LANES)

            @pl.loop(column, steps)
            def _(below):
                low = pl.ds(pl.multiple_of(below * LANES, LANES), LANES)
                for f in range(fronts):
                    work[f, low, side] = work[f, low, side] - dot_nt(
                        work[f, low, span], work[f, side, span]
                    )


def solve_rows(work, saved, lower):
    fronts, pivots, _ = work.shape
    for step in range(pivots // LANES):
        top = step * LANES
        for f in range(fronts):
            value = lower[f][:, top : top + LANES]
            if step:
                value = value - dot_nt(lower[f][:, :top], work[f, top : top + LANES, :top])
            lower[f][:, top : top + LANES] = dot_nt(value, saved[f, step])


def clear_upper(work, pivots):
    for step in range(pivots // LANES):
        top = step * LANES
        if top + LANES < pivots:
            for f in range(work.shape[0]):
                work[f, top : top + LANES, top + LANES : pivots] = jnp.zeros(
                    (LANES, pivots - top - LANES), jnp.float32
                )


def child_kernel(place, own, other, out, work, saved):
    core, live = place[0], place[1]
    slots, _, half, pivots = own.shape
    mine = pl.ds(pl.multiple_of(core * half, half), half)
    yours = pl.ds(pl.multiple_of((1 - core) * half, half), half)
    for s in range(slots):
        work[s, mine, :] = own[s, 0]
        work[s, yours, :] = other[s]
        out[s, 1] = own[s, 1]
    factor_pivots(work, saved)
    clear_upper(work, pivots)
    solve_rows(work, saved, [out.at[s, 1] for s in range(slots)])
    for s in range(slots):
        out[s, 0] = jnp.where(s < live, work[s, mine, :], 0.0)
        out[s, 1] = jnp.where(s < live, out[s, 1], 0.0)


def add_kernel(
    place, maps, own22, other22, own21, other21, parent, pivot_out, keep_out, send_out, whole
):
    core, live, half = place[0], place[1], place[2]
    slots, rows, width = own22.shape
    block = LANES
    per_core = rows // block
    blocks = width // block
    mine = pl.ds(pl.multiple_of(core * rows, rows), rows)
    yours = pl.ds(pl.multiple_of((1 - core) * rows, rows), rows)
    for s in range(slots):
        whole[s, mine, :] = own21[s]
        whole[s, yours, :] = other21[s]
    pivot_out[...] = jnp.zeros_like(pivot_out)
    keep_out[...] = parent[1]
    send_out[...] = jnp.zeros_like(send_out)
    pivot_out[half] = parent[0, :, : pivot_out.shape[2]]
    pivot_blocks = pivot_out.shape[2] // block

    @pl.loop(0, slots)
    def _(s):
        @pl.loop(0, blocks)
        def _(a):
            target = maps[s, a]

            @pl.when((s < live) & (target % 2 == core))
            def _():
                span = pl.ds(pl.multiple_of(a * block, block), block)
                low = pl.ds(pl.multiple_of((a % per_core) * block, block), block)
                is_mine = a // per_core == core
                source = jnp.where(is_mine, own22[s, low, :], other22[s, low, :])
                update = source - dot_nt(whole[s, span, :], whole[s])
                owner = (target // 2) % 2
                for b in range(blocks):
                    tile = update[:, b * block : (b + 1) * block]
                    column = maps[s, b]
                    there = pl.ds(pl.multiple_of(column * block, block), block)

                    @pl.when((target < pivot_blocks) & (column < pivot_blocks))
                    def _():
                        pivot_out[owner, :, there] += tile

                    @pl.when((target >= pivot_blocks) & (owner == half))
                    def _():
                        keep_out[:, there] += tile

                    @pl.when((target >= pivot_blocks) & (owner != half))
                    def _():
                        send_out[:, there] += tile


def parent_kernel(place, mine, yours, lower, out, work, saved):
    core, half = place[0], place[2]
    _, rows, pivots = mine.shape
    for h in range(2):
        work[0, pl.ds(pl.multiple_of((2 * h + core) * rows, rows), rows), :] = mine[h]
        work[0, pl.ds(pl.multiple_of((2 * h + 1 - core) * rows, rows), rows), :] = yours[h]
    out[1] = lower[...]
    factor_pivots(work, saved)
    clear_upper(work, pivots)
    solve_rows(work, saved, [out.at[1]])
    out[0] = work[0, pl.ds(pl.multiple_of((2 * half + core) * rows, rows), rows), :]


def update_kernel(place, base, own, mate, pair, cross, out):
    core, half = place[0], place[2]
    rows = own.shape[0]
    pieces = (
        (own, 2 * half + core),
        (mate, 2 * half + 1 - core),
        (pair, 2 * (1 - half) + core),
        (cross, 2 * (1 - half) + 1 - core),
    )
    for piece, index in pieces:
        side = pl.ds(pl.multiple_of(index * rows, rows), rows)
        out[:, side] = base[:, side] - dot_nt(own[...], piece[...])


def call(kernel, shapes, scratch, scalars, *arrays):
    vmem = pl.BlockSpec(memory_space=pltpu.VMEM)
    smem = pl.BlockSpec(memory_space=pltpu.SMEM)
    many = isinstance(shapes, list)
    made = [jax.ShapeDtypeStruct(s, jnp.float32) for s in (shapes if many else [shapes])]
    return pl.pallas_call(
        kernel,
        out_shape=made if many else made[0],
        in_specs=[smem] * len(scalars) + [vmem] * len(arrays),
        out_specs=[vmem] * len(made) if many else vmem,
        scratch_shapes=[pltpu.VMEM(s, jnp.float32) for s in scratch],
        compiler_params=pltpu.CompilerParams(vmem_limit_bytes=VMEM_LIMIT),
    )(*scalars, *arrays)


def on_device(child_fronts, child_live, row_map, parent_fronts):
    slots, _, quarter, order = child_fronts.shape
    pivots = order // 2
    core = lax.axis_index("front")
    half = lax.axis_index("leaf") % 2
    place = jnp.stack([core, child_live[0], half]).astype(jnp.int32)
    other_core = [(i, i ^ 1) for i in range(lax.axis_size("front"))]
    other_chip = [(i, i ^ 1) for i in range(lax.axis_size("leaf"))]

    def mate(x):
        return lax.ppermute(x, "front", other_core)

    def pair(x):
        return lax.ppermute(x, "leaf", other_chip)

    own_panel = child_fronts[:, :, :, :pivots]
    own22 = child_fronts[:, 1, :, pivots:]
    other_pivot = mate(child_fronts[:, 0, :, :pivots])
    other22 = mate(own22)
    child_panels = call(
        child_kernel,
        (slots, 2, quarter, pivots),
        [(slots, pivots, pivots), (slots, pivots // LANES, LANES, LANES)],
        [place],
        own_panel,
        other_pivot,
    )
    own21 = child_panels[:, 1]
    other21 = mate(own21)
    rows, parent_order = parent_fronts.shape[2:]
    parent_pivots = parent_order // 2
    pivot_part, keep, send = call(
        add_kernel,
        [(2, rows, parent_pivots), (rows, parent_order), (rows, parent_order)],
        [(slots, order - pivots, pivots)],
        [place, row_map],
        own22,
        other22,
        own21,
        other21,
        parent_fronts[0],
    )
    pivot_mine = pivot_part + pair(pivot_part)
    pivot_yours = mate(pivot_mine)
    lower = keep + pair(send)
    panel = call(
        parent_kernel,
        (2, rows, parent_pivots),
        [(1, parent_pivots, parent_pivots), (1, parent_pivots // LANES, LANES, LANES)],
        [place],
        pivot_mine,
        pivot_yours,
        lower[:, :parent_pivots],
    )
    lower21 = panel[1]
    from_pair = pair(lower21)
    update = call(
        update_kernel,
        (rows, parent_order - parent_pivots),
        [],
        [place],
        lower[:, parent_pivots:],
        lower21,
        mate(lower21),
        from_pair,
        mate(from_pair),
    )
    return child_panels, panel[None], update[None]


def solution(mesh):
    placed = (
        P("leaf", None, "front", None),
        P("leaf"),
        P("leaf", None),
        P("leaf", None, "front", None),
    )
    return jax.shard_map(
        on_device,
        mesh=mesh,
        in_specs=placed,
        out_specs=(
            P("leaf", None, "front", None),
            P("leaf", None, "front", None),
            P("leaf", "front", None),
        ),
        check_vma=False,
    )
```

```python
import functools

import jax
import jax.numpy as jnp
from jax import lax
from jax.experimental import pallas as pl
from jax.experimental.pallas import tpu as pltpu
from jax.sharding import PartitionSpec as P

LANES = 128
SUB = 8
GROUP = 4
PANEL = 32
VMEM_LIMIT = 60 * 1024 * 1024


def split(x):
    high = x.astype(jnp.bfloat16)
    return high, (x - high.astype(jnp.float32)).astype(jnp.bfloat16)


def dot_nt(a, b):
    a_high, a_low = split(a)
    b_high, b_low = split(b)
    return lax.dot_general(
        jnp.concatenate([a_high, a_high, a_low], axis=1),
        jnp.concatenate([b_high, b_low, b_high], axis=1),
        (((1,), (1,)), ((), ())),
        preferred_element_type=jnp.float32,
    )


def dot_nn(a, b):
    a_high, a_low = split(a)
    b_high, b_low = split(b)

    def one(x, y):
        return jnp.dot(x, y, preferred_element_type=jnp.float32)

    return one(a_high, b_high) + (one(a_high, b_low) + one(a_low, b_high))


def spread_lane(x, lane):
    return jnp.take_along_axis(x, jnp.full((SUB, LANES), lane, jnp.int32), 1, mode="promise_in_bounds")


def spread_row(x, row):
    return jnp.take_along_axis(x, jnp.full((SUB, LANES), row, jnp.int32), 0, mode="promise_in_bounds")


def eliminate_group(tiles, start, stop, lane_ids, row_ids):
    tile, first = divmod(start, SUB)
    size = GROUP
    rows = [spread_row(tiles[tile], first + k) for k in range(size)]
    heads = [spread_lane(tiles[tile], start + k) for k in range(size)]
    entry = {}
    for k in range(size):
        for l in range(k + 1):
            entry[k, l] = spread_row(heads[l], first + k)
    ratio = {}
    inverse = []
    for k in range(size):
        inverse.append(1.0 / entry[k, k])
        for m in range(k + 1, size):
            ratio[m, k] = entry[m, k] * inverse[k]
        for m in range(k + 1, size):
            for l in range(k + 1, m + 1):
                entry[m, l] = entry[m, l] - ratio[m, k] * entry[l, k]
    inside = (lane_ids >= start) & (lane_ids < start + size)
    for k in range(size):
        unit = jnp.where(lane_ids == start + k, 1.0, 0.0)
        rows[k] = jnp.where(inside, unit, rows[k])
    for k in range(size):
        for l in range(k):
            rows[k] = rows[k] - ratio[k, l] * rows[l]
    solved = [rows[k] * inverse[k] for k in range(size)]
    for k in range(size - 2, -1, -1):
        for m in range(k + 1, size):
            solved[k] = solved[k] - ratio[m, k] * solved[m]
    result = list(tiles)
    for t in range(tile, stop):
        old = tiles[t]
        if t == tile and first + size == SUB:
            new = old
        else:
            factors = [heads[k] if t == tile else spread_lane(old, start + k) for k in range(size)]
            new = jnp.where(inside, 0.0, old)
            for k in range(size):
                new = new - factors[k] * solved[k]
        if t == tile:
            new = jnp.where(row_ids < first, old, new)
            for k in range(size):
                root = lax.rsqrt(entry[k, k])
                new = jnp.where(row_ids == first + k, rows[k] * root, new)
        result[t] = new
    return result


def eliminate_below(tiles, low, stop):
    done = jnp.concatenate(tiles[low:stop], axis=0)
    below = jnp.concatenate(tiles[stop:], axis=0)
    lanes = lax.broadcasted_iota(jnp.int32, done.shape, 1)
    rows = lax.broadcasted_iota(jnp.int32, done.shape, 0)
    done = jnp.where((lanes > low * SUB + rows) & (lanes < stop * SUB), 0.0, done)
    lanes = lax.broadcasted_iota(jnp.int32, below.shape, 1)
    inside = (lanes >= low * SUB) & (lanes < stop * SUB)
    factors = dot_nt(jnp.where(inside, below, 0.0), done)
    below = jnp.where(inside, 0.0, below) - dot_nn(factors, done)
    count = len(tiles) - stop
    return tiles[:stop] + [below[t * SUB : (t + 1) * SUB, :] for t in range(count)]


def factor_inverses(blocks):
    lane_ids = lax.broadcasted_iota(jnp.int32, (SUB, LANES), 1)
    row_ids = lax.broadcasted_iota(jnp.int32, (SUB, LANES), 0)
    count = LANES // SUB
    tiles = [[b[t * SUB : (t + 1) * SUB, :] for t in range(count)] for b in blocks]
    panel = LANES if len(blocks) == 1 else PANEL
    for base in range(0, LANES, panel):
        low, stop = base // SUB, (base + panel) // SUB
        for start in range(base, base + panel, GROUP):
            tiles = [eliminate_group(t, start, stop, lane_ids, row_ids) for t in tiles]
        if stop < count:
            tiles = [eliminate_below(t, low, stop) for t in tiles]
    rows = lax.broadcasted_iota(jnp.int32, (LANES, LANES), 0)
    columns = lax.broadcasted_iota(jnp.int32, (LANES, LANES), 1)
    return [jnp.where(columns <= rows, jnp.concatenate(t, axis=0), 0.0) for t in tiles]


def factor_pivots(work, saved):
    fronts, pivots, _ = work.shape
    steps = pivots // LANES
    triangle = lax.broadcasted_iota(jnp.int32, (LANES, LANES), 1) <= lax.broadcasted_iota(
        jnp.int32, (LANES, LANES), 0
    )

    @pl.loop(0, steps)
    def _(step):
        span = pl.ds(pl.multiple_of(step * LANES, LANES), LANES)
        inverses = factor_inverses([work[f, span, span] for f in range(fronts)])
        for f in range(fronts):
            saved[f, step] = inverses[f]
            work[f, span, span] = jnp.where(
                triangle, dot_nt(work[f, span, span], inverses[f]), 0.0
            )

        @pl.loop(step + 1, steps)
        def _(below):
            low = pl.ds(pl.multiple_of(below * LANES, LANES), LANES)
            for f in range(fronts):
                work[f, low, span] = dot_nt(work[f, low, span], saved[f, step])

        @pl.loop(step + 1, steps)
        def _(column):
            side = pl.ds(pl.multiple_of(column * LANES, LANES), LANES)

            @pl.loop(column, steps)
            def _(below):
                low = pl.ds(pl.multiple_of(below * LANES, LANES), LANES)
                for f in range(fronts):
                    work[f, low, side] = work[f, low, side] - dot_nt(
                        work[f, low, span], work[f, side, span]
                    )


def solve_rows(work, saved, lower):
    fronts, pivots, _ = work.shape
    for step in range(pivots // LANES):
        top = step * LANES
        for f in range(fronts):
            value = lower[f][:, top : top + LANES]
            if step:
                value = value - dot_nt(lower[f][:, :top], work[f, top : top + LANES, :top])
            lower[f][:, top : top + LANES] = dot_nt(value, saved[f, step])


def clear_upper(work, pivots):
    for step in range(pivots // LANES):
        top = step * LANES
        if top + LANES < pivots:
            for f in range(work.shape[0]):
                work[f, top : top + LANES, top + LANES : pivots] = jnp.zeros(
                    (LANES, pivots - top - LANES), jnp.float32
                )


def child_kernel(place, own, other, out, work, saved):
    core, live = place[0], place[1]
    slots, _, half, pivots = own.shape
    mine = pl.ds(pl.multiple_of(core * half, half), half)
    yours = pl.ds(pl.multiple_of((1 - core) * half, half), half)
    for s in range(slots):
        work[s, mine, :] = own[s, 0]
        work[s, yours, :] = other[s]
        out[s, 1] = own[s, 1]
    factor_pivots(work, saved)
    clear_upper(work, pivots)
    solve_rows(work, saved, [out.at[s, 1] for s in range(slots)])
    for s in range(slots):
        out[s, 0] = jnp.where(s < live, work[s, mine, :], 0.0)
        out[s, 1] = jnp.where(s < live, out[s, 1], 0.0)


def add_kernel(
    place, maps, own22, other22, own21, other21, parent, pivot_out, keep_out, send_out, whole
):
    core, live, half = place[0], place[1], place[2]
    slots, rows, width = own22.shape
    block = LANES
    per_core = rows // block
    blocks = width // block
    mine = pl.ds(pl.multiple_of(core * rows, rows), rows)
    yours = pl.ds(pl.multiple_of((1 - core) * rows, rows), rows)
    for s in range(slots):
        whole[s, mine, :] = own21[s]
        whole[s, yours, :] = other21[s]
    pivot_out[...] = jnp.zeros_like(pivot_out)
    keep_out[...] = parent[1]
    send_out[...] = jnp.zeros_like(send_out)
    pivot_out[half] = parent[0, :, : pivot_out.shape[2]]
    pivot_blocks = pivot_out.shape[2] // block

    @pl.loop(0, slots)
    def _(s):
        @pl.loop(0, blocks)
        def _(a):
            target = maps[s, a]

            @pl.when((s < live) & (target % 2 == core))
            def _():
                span = pl.ds(pl.multiple_of(a * block, block), block)
                low = pl.ds(pl.multiple_of((a % per_core) * block, block), block)
                is_mine = a // per_core == core
                source = jnp.where(is_mine, own22[s, low, :], other22[s, low, :])
                update = source - dot_nt(whole[s, span, :], whole[s])
                owner = (target // 2) % 2
                for b in range(blocks):
                    tile = update[:, b * block : (b + 1) * block]
                    column = maps[s, b]
                    there = pl.ds(pl.multiple_of(column * block, block), block)

                    @pl.when((target < pivot_blocks) & (column < pivot_blocks))
                    def _():
                        pivot_out[owner, :, there] += tile

                    @pl.when((target >= pivot_blocks) & (owner == half))
                    def _():
                        keep_out[:, there] += tile

                    @pl.when((target >= pivot_blocks) & (owner != half))
                    def _():
                        send_out[:, there] += tile


def parent_kernel(place, mine, yours, lower, out, work, saved):
    core, half = place[0], place[2]
    _, rows, pivots = mine.shape
    for h in range(2):
        work[0, pl.ds(pl.multiple_of((2 * h + core) * rows, rows), rows), :] = mine[h]
        work[0, pl.ds(pl.multiple_of((2 * h + 1 - core) * rows, rows), rows), :] = yours[h]
    out[1] = lower[...]
    factor_pivots(work, saved)
    clear_upper(work, pivots)
    solve_rows(work, saved, [out.at[1]])
    out[0] = work[0, pl.ds(pl.multiple_of((2 * half + core) * rows, rows), rows), :]


def update_kernel(place, base, own, mate, pair, cross, out):
    core, half = place[0], place[2]
    rows = own.shape[0]
    pieces = (
        (own, 2 * half + core),
        (mate, 2 * half + 1 - core),
        (pair, 2 * (1 - half) + core),
        (cross, 2 * (1 - half) + 1 - core),
    )
    for piece, index in pieces:
        side = pl.ds(pl.multiple_of(index * rows, rows), rows)
        out[:, side] = base[:, side] - dot_nt(own[...], piece[...])


def call(kernel, shapes, scratch, scalars, *arrays):
    vmem = pl.BlockSpec(memory_space=pltpu.VMEM)
    smem = pl.BlockSpec(memory_space=pltpu.SMEM)
    many = isinstance(shapes, list)
    made = [jax.ShapeDtypeStruct(s, jnp.float32) for s in (shapes if many else [shapes])]
    return pl.pallas_call(
        kernel,
        out_shape=made if many else made[0],
        in_specs=[smem] * len(scalars) + [vmem] * len(arrays),
        out_specs=[vmem] * len(made) if many else vmem,
        scratch_shapes=[pltpu.VMEM(s, jnp.float32) for s in scratch],
        compiler_params=pltpu.CompilerParams(vmem_limit_bytes=VMEM_LIMIT),
    )(*scalars, *arrays)


def on_device(child_fronts, child_live, row_map, parent_fronts):
    slots, _, quarter, order = child_fronts.shape
    pivots = order // 2
    core = lax.axis_index("front")
    half = lax.axis_index("leaf") % 2
    place = jnp.stack([core, child_live[0], half]).astype(jnp.int32)
    other_core = [(i, i ^ 1) for i in range(lax.axis_size("front"))]
    other_chip = [(i, i ^ 1) for i in range(lax.axis_size("leaf"))]

    def mate(x):
        return lax.ppermute(x, "front", other_core)

    def pair(x):
        return lax.ppermute(x, "leaf", other_chip)

    own_panel = child_fronts[:, :, :, :pivots]
    own22 = child_fronts[:, 1, :, pivots:]
    other_pivot = mate(child_fronts[:, 0, :, :pivots])
    other22 = mate(own22)
    child_panels = call(
        child_kernel,
        (slots, 2, quarter, pivots),
        [(slots, pivots, pivots), (slots, pivots // LANES, LANES, LANES)],
        [place],
        own_panel,
        other_pivot,
    )
    own21 = child_panels[:, 1]
    other21 = mate(own21)
    rows, parent_order = parent_fronts.shape[2:]
    parent_pivots = parent_order // 2
    pivot_part, keep, send = call(
        add_kernel,
        [(2, rows, parent_pivots), (rows, parent_order), (rows, parent_order)],
        [(slots, order - pivots, pivots)],
        [place, row_map],
        own22,
        other22,
        own21,
        other21,
        parent_fronts[0],
    )
    pivot_mine = pivot_part + pair(pivot_part)
    pivot_yours = mate(pivot_mine)
    lower = keep + pair(send)
    panel = call(
        parent_kernel,
        (2, rows, parent_pivots),
        [(1, parent_pivots, parent_pivots), (1, parent_pivots // LANES, LANES, LANES)],
        [place],
        pivot_mine,
        pivot_yours,
        lower[:, :parent_pivots],
    )
    lower21 = panel[1]
    from_pair = pair(lower21)
    update = call(
        update_kernel,
        (rows, parent_order - parent_pivots),
        [],
        [place],
        lower[:, parent_pivots:],
        lower21,
        mate(lower21),
        from_pair,
        mate(from_pair),
    )
    return child_panels, panel[None], update[None]


def solution(mesh):
    placed = (
        P("leaf", None, "front", None),
        P("leaf"),
        P("leaf", None),
        P("leaf", None, "front", None),
    )
    return jax.shard_map(
        on_device,
        mesh=mesh,
        in_specs=placed,
        out_specs=(
            P("leaf", None, "front", None),
            P("leaf", None, "front", None),
            P("leaf", "front", None),
        ),
        check_vma=False,
    )
```

```python
import functools

import jax
import jax.numpy as jnp
from jax import lax
from jax.experimental import pallas as pl
from jax.experimental.pallas import tpu as pltpu
from jax.sharding import PartitionSpec as P

LANES = 128
SUB = 8
GROUP = 4
PANEL = 32
VMEM_LIMIT = 60 * 1024 * 1024


def split(x):
    high = x.astype(jnp.bfloat16)
    return high, (x - high.astype(jnp.float32)).astype(jnp.bfloat16)


def dot_nt(a, b):
    a_high, a_low = split(a)
    b_high, b_low = split(b)
    return lax.dot_general(
        jnp.concatenate([a_high, a_high, a_low], axis=1),
        jnp.concatenate([b_high, b_low, b_high], axis=1),
        (((1,), (1,)), ((), ())),
        preferred_element_type=jnp.float32,
    )


def dot_nn(a, b):
    a_high, a_low = split(a)
    b_high, b_low = split(b)

    def one(x, y):
        return jnp.dot(x, y, preferred_element_type=jnp.float32)

    return one(a_high, b_high) + (one(a_high, b_low) + one(a_low, b_high))


def spread_lane(x, lane):
    return jnp.take_along_axis(x, jnp.full((SUB, LANES), lane, jnp.int32), 1, mode="promise_in_bounds")


def spread_row(x, row):
    return jnp.take_along_axis(x, jnp.full((SUB, LANES), row, jnp.int32), 0, mode="promise_in_bounds")


def eliminate_group(tiles, start, stop, lane_ids, row_ids):
    tile, first = divmod(start, SUB)
    size = GROUP
    rows = [spread_row(tiles[tile], first + k) for k in range(size)]
    heads = [spread_lane(tiles[tile], start + k) for k in range(size)]
    entry = {}
    for k in range(size):
        for l in range(k + 1):
            entry[k, l] = spread_row(heads[l], first + k)
    ratio = {}
    inverse = []
    for k in range(size):
        inverse.append(1.0 / entry[k, k])
        for m in range(k + 1, size):
            ratio[m, k] = entry[m, k] * inverse[k]
        for m in range(k + 1, size):
            for l in range(k + 1, m + 1):
                entry[m, l] = entry[m, l] - ratio[m, k] * entry[l, k]
    inside = (lane_ids >= start) & (lane_ids < start + size)
    for k in range(size):
        unit = jnp.where(lane_ids == start + k, 1.0, 0.0)
        rows[k] = jnp.where(inside, unit, rows[k])
    for k in range(size):
        for l in range(k):
            rows[k] = rows[k] - ratio[k, l] * rows[l]
    solved = [rows[k] * inverse[k] for k in range(size)]
    for k in range(size - 2, -1, -1):
        for m in range(k + 1, size):
            solved[k] = solved[k] - ratio[m, k] * solved[m]
    result = list(tiles)
    for t in range(tile, stop):
        old = tiles[t]
        if t == tile and first + size == SUB:
            new = old
        else:
            factors = [heads[k] if t == tile else spread_lane(old, start + k) for k in range(size)]
            new = jnp.where(inside, 0.0, old)
            for k in range(size):
                new = new - factors[k] * solved[k]
        if t == tile:
            new = jnp.where(row_ids < first, old, new)
            for k in range(size):
                root = lax.rsqrt(entry[k, k])
                new = jnp.where(row_ids == first + k, rows[k] * root, new)
        result[t] = new
    return result


def eliminate_below(tiles, low, stop):
    done = jnp.concatenate(tiles[low:stop], axis=0)
    below = jnp.concatenate(tiles[stop:], axis=0)
    lanes = lax.broadcasted_iota(jnp.int32, done.shape, 1)
    rows = lax.broadcasted_iota(jnp.int32, done.shape, 0)
    done = jnp.where((lanes > low * SUB + rows) & (lanes < stop * SUB), 0.0, done)
    lanes = lax.broadcasted_iota(jnp.int32, below.shape, 1)
    inside = (lanes >= low * SUB) & (lanes < stop * SUB)
    factors = dot_nt(jnp.where(inside, below, 0.0), done)
    below = jnp.where(inside, 0.0, below) - dot_nn(factors, done)
    count = len(tiles) - stop
    return tiles[:stop] + [below[t * SUB : (t + 1) * SUB, :] for t in range(count)]


def factor_inverses(blocks):
    lane_ids = lax.broadcasted_iota(jnp.int32, (SUB, LANES), 1)
    row_ids = lax.broadcasted_iota(jnp.int32, (SUB, LANES), 0)
    count = LANES // SUB
    tiles = [[b[t * SUB : (t + 1) * SUB, :] for t in range(count)] for b in blocks]
    panel = LANES if len(blocks) == 1 else PANEL
    for base in range(0, LANES, panel):
        low, stop = base // SUB, (base + panel) // SUB
        for start in range(base, base + panel, GROUP):
            tiles = [eliminate_group(t, start, stop, lane_ids, row_ids) for t in tiles]
        if stop < count:
            tiles = [eliminate_below(t, low, stop) for t in tiles]
    rows = lax.broadcasted_iota(jnp.int32, (LANES, LANES), 0)
    columns = lax.broadcasted_iota(jnp.int32, (LANES, LANES), 1)
    return [jnp.where(columns <= rows, jnp.concatenate(t, axis=0), 0.0) for t in tiles]


def factor_pivots(work, saved):
    fronts, pivots, _ = work.shape
    steps = pivots // LANES
    triangle = lax.broadcasted_iota(jnp.int32, (LANES, LANES), 1) <= lax.broadcasted_iota(
        jnp.int32, (LANES, LANES), 0
    )

    @pl.loop(0, steps)
    def _(step):
        span = pl.ds(pl.multiple_of(step * LANES, LANES), LANES)
        inverses = factor_inverses([work[f, span, span] for f in range(fronts)])
        for f in range(fronts):
            saved[f, step] = inverses[f]
            work[f, span, span] = jnp.where(
                triangle, dot_nt(work[f, span, span], inverses[f]), 0.0
            )

        @pl.loop(step + 1, steps)
        def _(below):
            low = pl.ds(pl.multiple_of(below * LANES, LANES), LANES)
            for f in range(fronts):
                work[f, low, span] = dot_nt(work[f, low, span], saved[f, step])

        @pl.loop(step + 1, steps)
        def _(column):
            side = pl.ds(pl.multiple_of(column * LANES, LANES), LANES)

            @pl.loop(column, steps)
            def _(below):
                low = pl.ds(pl.multiple_of(below * LANES, LANES), LANES)
                for f in range(fronts):
                    work[f, low, side] = work[f, low, side] - dot_nt(
                        work[f, low, span], work[f, side, span]
                    )


def solve_rows(work, saved, lower):
    fronts, pivots, _ = work.shape
    for step in range(pivots // LANES):
        top = step * LANES
        for f in range(fronts):
            value = lower[f][:, top : top + LANES]
            if step:
                value = value - dot_nt(lower[f][:, :top], work[f, top : top + LANES, :top])
            lower[f][:, top : top + LANES] = dot_nt(value, saved[f, step])


def clear_upper(work, pivots):
    for step in range(pivots // LANES):
        top = step * LANES
        if top + LANES < pivots:
            for f in range(work.shape[0]):
                work[f, top : top + LANES, top + LANES : pivots] = jnp.zeros(
                    (LANES, pivots - top - LANES), jnp.float32
                )


def child_kernel(place, own, other, out, work, saved):
    core, live = place[0], place[1]
    slots, _, half, pivots = own.shape
    mine = pl.ds(pl.multiple_of(core * half, half), half)
    yours = pl.ds(pl.multiple_of((1 - core) * half, half), half)
    for s in range(slots):
        work[s, mine, :] = own[s, 0]
        work[s, yours, :] = other[s]
        out[s, 1] = own[s, 1]
    factor_pivots(work, saved)
    clear_upper(work, pivots)
    solve_rows(work, saved, [out.at[s, 1] for s in range(slots)])
    for s in range(slots):
        out[s, 0] = jnp.where(s < live, work[s, mine, :], 0.0)
        out[s, 1] = jnp.where(s < live, out[s, 1], 0.0)


def add_kernel(
    place, maps, own22, other22, own21, other21, parent, pivot_out, keep_out, send_out, whole
):
    core, live, half = place[0], place[1], place[2]
    slots, rows, width = own22.shape
    block = LANES
    per_core = rows // block
    blocks = width // block
    mine = pl.ds(pl.multiple_of(core * rows, rows), rows)
    yours = pl.ds(pl.multiple_of((1 - core) * rows, rows), rows)
    for s in range(slots):
        whole[s, mine, :] = own21[s]
        whole[s, yours, :] = other21[s]
    pivot_out[...] = jnp.zeros_like(pivot_out)
    keep_out[...] = parent[1]
    send_out[...] = jnp.zeros_like(send_out)
    pivots = parent.shape[2] // 2
    first = pivots // 2
    pivot_blocks = pivots // block

    @pl.when(half == 0)
    def _():
        pivot_out[:, :first] = parent[0, :, :first]

    @pl.when(half == 1)
    def _():
        pivot_out[:, first:] = parent[0, :, :pivots]


    @pl.loop(0, slots)
    def _(s):
        @pl.loop(0, blocks)
        def _(a):
            target = maps[s, a]

            @pl.when((s < live) & (target % 2 == core))
            def _():
                span = pl.ds(pl.multiple_of(a * block, block), block)
                low = pl.ds(pl.multiple_of((a % per_core) * block, block), block)
                is_mine = a // per_core == core
                source = jnp.where(is_mine, own22[s, low, :], other22[s, low, :])
                update = source - dot_nt(whole[s, span, :], whole[s])
                owner = (target // 2) % 2
                for b in range(blocks):
                    tile = update[:, b * block : (b + 1) * block]
                    column = maps[s, b]
                    there = pl.ds(pl.multiple_of(column * block, block), block)

                    packed = pl.ds(pl.multiple_of(owner * first + column * block, block), block)

                    @pl.when((target < pivot_blocks) & (column <= target))
                    def _():
                        pivot_out[:, packed] += tile

                    @pl.when((target >= pivot_blocks) & (owner == half))
                    def _():
                        keep_out[:, there] += tile

                    @pl.when((target >= pivot_blocks) & (owner != half))
                    def _():
                        send_out[:, there] += tile


def parent_kernel(place, mine, yours, out, work, saved):
    core, half = place[0], place[2]
    rows = mine.shape[0]
    pivots = out.shape[1]
    first = pivots // 2
    for source, side in ((mine, core), (yours, 1 - core)):
        low = pl.ds(pl.multiple_of(side * rows, rows), rows)
        high = pl.ds(pl.multiple_of((2 + side) * rows, rows), rows)
        work[0, low, :first] = source[:, :first]
        work[0, high, :] = source[:, first:]
    factor_pivots(work, saved)
    clear_upper(work, pivots)
    out[...] = work[0, pl.ds(pl.multiple_of((2 * half + core) * rows, rows), rows), :]


def lower_kernel(work, saved, keep, received, out, rest):
    pivots = out.shape[1]
    out[...] = keep[:, :pivots] + received[:, :pivots]
    rest[...] = keep[:, pivots:] + received[:, pivots:]
    solve_rows(work, saved, [out])


def update_kernel(place, base, own, mate, pair, cross, out):
    core, half = place[0], place[2]
    rows = own.shape[0]
    pieces = (
        (own, 2 * half + core),
        (mate, 2 * half + 1 - core),
        (pair, 2 * (1 - half) + core),
        (cross, 2 * (1 - half) + 1 - core),
    )
    for piece, index in pieces:
        side = pl.ds(pl.multiple_of(index * rows, rows), rows)
        out[:, side] = base[:, side] - dot_nt(own[...], piece[...])


def call(kernel, shapes, scratch, scalars, *arrays):
    vmem = pl.BlockSpec(memory_space=pltpu.VMEM)
    smem = pl.BlockSpec(memory_space=pltpu.SMEM)
    many = isinstance(shapes, list)
    made = [jax.ShapeDtypeStruct(s, jnp.float32) for s in (shapes if many else [shapes])]
    return pl.pallas_call(
        kernel,
        out_shape=made if many else made[0],
        in_specs=[smem] * len(scalars) + [vmem] * len(arrays),
        out_specs=[vmem] * len(made) if many else vmem,
        scratch_shapes=[pltpu.VMEM(s, jnp.float32) for s in scratch],
        compiler_params=pltpu.CompilerParams(vmem_limit_bytes=VMEM_LIMIT),
    )(*scalars, *arrays)


def on_device(child_fronts, child_live, row_map, parent_fronts):
    slots, _, quarter, order = child_fronts.shape
    pivots = order // 2
    core = lax.axis_index("front")
    half = lax.axis_index("leaf") % 2
    place = jnp.stack([core, child_live[0], half]).astype(jnp.int32)
    other_core = [(i, i ^ 1) for i in range(lax.axis_size("front"))]
    other_chip = [(i, i ^ 1) for i in range(lax.axis_size("leaf"))]

    def mate(x):
        return lax.ppermute(x, "front", other_core)

    def pair(x):
        return lax.ppermute(x, "leaf", other_chip)

    own_panel = child_fronts[:, :, :, :pivots]
    own22 = child_fronts[:, 1, :, pivots:]
    other_pivot = mate(child_fronts[:, 0, :, :pivots])
    other22 = mate(own22)
    child_panels = call(
        child_kernel,
        (slots, 2, quarter, pivots),
        [(slots, pivots, pivots), (slots, pivots // LANES, LANES, LANES)],
        [place],
        own_panel,
        other_pivot,
    )
    own21 = child_panels[:, 1]
    other21 = mate(own21)
    rows, parent_order = parent_fronts.shape[2:]
    parent_pivots = parent_order // 2
    pivot_part, keep, send = call(
        add_kernel,
        [(rows, parent_pivots + parent_pivots // 2), (rows, parent_order), (rows, parent_order)],
        [(slots, order - pivots, pivots)],
        [place, row_map],
        own22,
        other22,
        own21,
        other21,
        parent_fronts[0],
    )
    pivot_received, send = lax.optimization_barrier((pair(pivot_part), send))
    pivot_mine = pivot_part + pivot_received
    pivot_yours = mate(pivot_mine)
    received = pair(send)
    steps = parent_pivots // LANES
    factor, work, saved = call(
        parent_kernel,
        [(rows, parent_pivots), (1, parent_pivots, parent_pivots), (1, steps, LANES, LANES)],
        [],
        [place],
        pivot_mine,
        pivot_yours,
    )
    lower21, rest = call(
        lower_kernel,
        [(rows, parent_pivots), (rows, parent_order - parent_pivots)],
        [],
        [],
        work,
        saved,
        keep,
        received,
    )
    panel = jnp.stack([factor, lower21])
    from_pair = pair(lower21)
    update = call(
        update_kernel,
        (rows, parent_order - parent_pivots),
        [],
        [place],
        rest,
        lower21,
        mate(lower21),
        from_pair,
        mate(from_pair),
    )
    return child_panels, panel[None], update[None]


def solution(mesh):
    placed = (
        P("leaf", None, "front", None),
        P("leaf"),
        P("leaf", None),
        P("leaf", None, "front", None),
    )
    return jax.shard_map(
        on_device,
        mesh=mesh,
        in_specs=placed,
        out_specs=(
            P("leaf", None, "front", None),
            P("leaf", None, "front", None),
            P("leaf", "front", None),
        ),
        check_vma=False,
    )
```
